512 devices in a mesh: req: 16 (over z), ctx: 32 (over x, y, core).
Axes of the slice: x: 4, y: 4, z: 16, core: 2. Of those that a mesh axis runs over, the one named last changes fastest.
Arguments:
- query_rows: bfloat16 [131072, 1024], P(('req', 'ctx')), parts along dimension 0, may hold values from -8 to 8
- key_rows: bfloat16 [131072, 128], P(('req', 'ctx')), parts along dimension 0, may hold values from -8 to 8
- value_rows: bfloat16 [131072, 128], P(('req', 'ctx')), parts along dimension 0, may hold values from -8 to 8
- document_ids: int32 [131072], P('req'), parts along dimension 0, may hold values from 0 to 7, never falling along the last dimension, each value on 1 to 4096 neighbouring positions
Outputs:
- attended: bfloat16 [131072, 1024], P(('req', 'ctx')), parts along dimension 0
The draws below stay inside these ranges and needn't reach their ends.
There are 16 independent parts, one for each index of `req`. The reference program is written for one: setup_inputs(seed, part) draws one part's arguments, and reference() takes and returns one part's arrays. A program takes and returns all parts, laid end to end along the dimension named above; each array names one. Nothing has to cross between parts.
All inputs are finite; a program needn't handle non-finite values.
Results may differ from the reference program's by a relative error of at most 0.004.
Values may be sent and summed in bfloat16 or wider, within the bound.
No kernel may reach another device: no remote copies, remote signals or barrier semaphores. Data moves between devices by JAX's collectives and lax.ppermute only.
A program may use at most 64 MiB of HBM per device.

```python
import math
import jax
import jax.numpy as jnp
import numpy as np
from jax import lax

HEADS = 8
HEAD_DIM = 128
DOCS = 8
TOKENS = 8192
DOC_MOST = 4096


def base_noise(key, columns):
    return jnp.clip(jax.random.normal(key, (TOKENS, columns), jnp.float32), -6.0, 6.0)


def draw_key_rows(key, part):
    noise = base_noise(jax.random.fold_in(key, 2), HEAD_DIM)
    return noise.astype(jnp.bfloat16)


def draw_query_rows(key, part):
    noise = base_noise(jax.random.fold_in(key, 1), HEADS * HEAD_DIM)
    return noise.astype(jnp.bfloat16)


def block_scale(rng, shape, pieces, least, top_value):
    level = 1.0
    for dim, blocks in pieces:
        steps = jax.random.uniform(jax.random.fold_in(jax.random.fold_in(rng, 6), dim), (blocks,), jnp.float32, least / len(pieces), top_value / len(pieces))
        level = level * jnp.repeat(jnp.exp(steps), shape[dim] // blocks).reshape((-1,) + (1,) * (len(shape) - 1 - dim))
    return level


def length_profile(number_of, total, reach, slope):
    weights = [(1 << 20) // math.isqrt(standing ** slope) + 1 for standing in range(2, number_of + 1)]
    surplus, given = total - reach - (number_of - 1), [1] * (number_of - 1)
    while surplus > 0:
        candidates = [i for i in range(number_of - 1) if given[i] < reach]
        pool, left = sum([weights[i] for i in candidates]), surplus
        for i in candidates:
            more = min(reach - given[i], max(1, left * weights[i] // pool), surplus)
            given[i] = given[i] + more
            surplus = surplus - more
    return np.array([reach] + given)


def uneven(key, count, total, limit, skew):
    if count == 2:
        one = jax.random.randint(key, (), max(1, total - limit), min(limit, total - 1) + 1)
        return jnp.stack([one, total - one])
    tallies = jnp.asarray(length_profile(count, total, limit, skew), jnp.int32)
    pairs = (count - 1) // 2
    source_of, sink = tallies[1:1 + 2 * pairs:2], tallies[2:2 + 2 * pairs:2]
    slack = jnp.minimum(source_of - 1, limit - sink)
    passed = jax.random.randint(jax.random.fold_in(key, 1), (pairs,), 0, 1 << 20) % (slack + 1)
    tallies = tallies.at[1:1 + 2 * pairs:2].set(source_of - passed).at[2:2 + 2 * pairs:2].set(sink + passed)
    return tallies[jax.random.permutation(jax.random.fold_in(key, 2), count)]


def scatter_about(own_key, shape, scale, most, shards=(), kind=jnp.bfloat16):
    level = block_scale(own_key, shape, shards, -0.22, 0.18) if shards else 1.0
    array = jax.random.normal(own_key, shape, jnp.float32) * scale * level
    return jnp.minimum(jnp.maximum(array, -most), most).astype(kind)


def setup_inputs(seed: int = 0, part: int = 0) -> dict:
    seeds = jax.random.split(jax.random.key(seed), 5)
    part_splits = jax.random.split(jax.random.fold_in(seeds[4], part), 5)
    query_rows = draw_query_rows(jax.random.fold_in(jax.random.fold_in(seeds[4], part), 71), part)
    key_rows = draw_key_rows(jax.random.fold_in(jax.random.fold_in(seeds[4], part), 71), part)
    value_rows = scatter_about(part_splits[2], (TOKENS, HEAD_DIM), 2.0, 8.0, ((0, 32),))
    document_ids = jnp.searchsorted(jnp.cumsum(uneven(part_splits[3], DOCS, TOKENS, DOC_MOST, 1)), jnp.arange(TOKENS), side="right").astype(jnp.int32)
    return {"query_rows": query_rows, "key_rows": key_rows, "value_rows": value_rows, "document_ids": document_ids}


def reference(query_rows, key_rows, value_rows, document_ids):
    block = math.gcd(TOKENS, 512)
    stacked = query_rows.reshape(TOKENS, HEADS, HEAD_DIM).astype(jnp.float32)
    key_float = key_rows.astype(jnp.float32)
    value_float = value_rows.astype(jnp.float32)
    key_positions = jnp.arange(TOKENS, dtype=jnp.int32)
    factor = 1.0 / math.sqrt(HEAD_DIM)

    def one_block(which):
        first = (which * block).astype(jnp.int32)
        query_block = lax.dynamic_slice_in_dim(stacked, first, block, 0)
        query_positions = first + jnp.arange(block, dtype=jnp.int32)
        query_docs = lax.dynamic_slice_in_dim(document_ids, first, block, 0)
        scores = jnp.einsum('thd,sd->ths', query_block, key_float) * factor
        allowed = (query_docs[:, None] == document_ids[None, :]) & (key_positions[None, :] <= query_positions[:, None])
        masked = jnp.where(allowed[:, None, :], scores, jnp.float32(-1e+30))
        largest = lax.optimization_barrier(jnp.max(masked, axis=-1))
        weights = jnp.where(allowed[:, None, :], jnp.exp(masked - largest[..., None]), jnp.float32(0.0))
        totals = lax.optimization_barrier(jnp.sum(weights, axis=-1))
        rounded = lax.optimization_barrier(weights.astype(jnp.bfloat16))
        numerator = jnp.einsum('ths,sd->thd', rounded.astype(jnp.float32), value_float)
        result = numerator / totals[..., None]
        return result.reshape(block, HEADS * HEAD_DIM).astype(jnp.bfloat16)
    blocks = lax.map(one_block, jnp.arange(TOKENS // block, dtype=jnp.int32))
    return blocks.reshape(TOKENS, HEADS * HEAD_DIM)
```

```python
import functools
import math

import jax
import jax.numpy as jnp
from jax import lax
from jax.experimental import pallas as pl
from jax.experimental.pallas import tpu as pltpu
from jax.sharding import PartitionSpec as P


HEADS = 8
DIM = 128
ROWS = 256
SIDE = 4
DOCS = 8
SCALE = math.log2(math.e) / math.sqrt(DIM)
NEG = -1e30
ORDER = (8, 7, 6, 5, 4, 3, 2, 1)
EARLY = (8, 7, 6, 5)
LATE = (4, 3, 2, 1)
GRANT = 32 << 20
VM = pl.BlockSpec(memory_space=pltpu.VMEM)


SM = pl.BlockSpec(memory_space=pltpu.SMEM)


def start_of(positions, bounds):
    start = jnp.zeros_like(positions)
    for b in bounds:
        start = jnp.where(positions >= b, jnp.maximum(start, b), start)
    return start


def score(q, keys, mask):
    scores = [
        lax.dot_general(q, k, (((1,), (1,)), ((), ())), preferred_element_type=jnp.float32)
        for k in keys
    ]
    if mask is None:
        return scores
    return [jnp.where(ok, s, NEG) for s, ok in zip(scores, mask)]


def absorb(h, scores, values, rows_ok, old_state, state):
    top = jnp.max(functools.reduce(jnp.maximum, scores), axis=1, keepdims=True)
    m_ref, l_ref, acc_ref = state
    if rows_ok is not None:
        top = jnp.where(rows_ok, top, NEG)
    if old_state is None:
        new = jnp.broadcast_to(top, (ROWS, DIM))
    else:
        old_m, old_l, old_acc = old_state
        old = old_m[h]
        new = jnp.maximum(old, top)
    cut = new * SCALE
    if rows_ok is not None:
        cut = jnp.where(rows_ok, cut, -NEG)
    wide = jnp.concatenate([cut] * (ROWS // DIM), axis=1)
    total = None
    for s, v in zip(scores, values):
        p = jnp.exp2(s * SCALE - wide).astype(jnp.bfloat16)
        part = jnp.dot(p, v, preferred_element_type=jnp.float32)
        total = part if total is None else total + part
    if old_state is None:
        acc_ref[h] = total[:, :DIM]
        l_ref[h] = total[:, DIM:]
    else:
        shrink = jnp.exp2((old - new) * SCALE)
        acc_ref[h] = old_acc[h] * shrink + total[:, :DIM]
        l_ref[h] = old_l[h] * shrink + total[:, DIM:]
    m_ref[h] = new


def all_heads(q_ref, keys, values, mask, rows_ok, old_state, state):
    values = [jnp.concatenate([v, jnp.ones_like(v)], axis=1) for v in values]
    ahead = len(keys) > 2
    scores = [None] * (HEADS + 1)

    def fill(h):
        if h < HEADS and scores[h] is None:
            scores[h] = score(q_ref[:, h * DIM : (h + 1) * DIM], keys, mask)

    for h in range(HEADS):
        fill(h)
        if ahead:
            fill(h + 1)
        absorb(h, scores[h], values, rows_ok, old_state, state)
        scores[h] = ()


def own_kernel(ids_ref, q_ref, kv_ref, m_ref, l_ref, acc_ref, bounds_ref):
    block = lax.axis_index("ctx")
    base = block * ROWS
    ids = ids_ref[...]
    bounds = [jnp.sum((ids < d).astype(jnp.int32)) for d in range(1, DOCS)]
    for i, b in enumerate(bounds):
        bounds_ref[i] = b
    rows = base + lax.broadcasted_iota(jnp.int32, (ROWS, ROWS), 0)
    cols = base + lax.broadcasted_iota(jnp.int32, (ROWS, ROWS), 1)
    mask = (cols <= rows) & (cols >= start_of(rows, bounds))
    k, v = kv_ref[pl.ds(0, ROWS), :], kv_ref[pl.ds(ROWS, ROWS), :]
    all_heads(q_ref, [k], [v], [mask], None, None, (m_ref, l_ref, acc_ref))


def far_kernel(places, sides, seeds, pack, bounds_ref, *refs):
    q_refs, refs = refs[: len(sides)], refs[len(sides) :]
    n = 1 + max(i for i, _, _ in places)
    sets, refs = refs[:n], refs[n:]
    olds = []
    for seed in seeds:
        olds.append(None if seed else refs[:3])
        refs = refs if seed else refs[3:]
    if pack:
        packed_ref, refs = refs[0], refs[1:]
    block = lax.axis_index("ctx")
    bounds = [bounds_ref[i] for i in range(DOCS - 1)]
    where = [jnp.int32(blk(block)) for _, _, blk in places]
    for j, side in enumerate(sides):
        state, old, q_ref = refs[3 * j : 3 * j + 3], olds[j], q_refs[j]
        mine = block + side * (1 - 2 * lax.rem(block, 2))
        base = mine * ROWS
        start = start_of(base, bounds)
        live = [(w >= 0) & (w < mine) & (w * ROWS + ROWS > start) for w in where]
        alive = functools.reduce(jnp.logical_or, live)
        whole = functools.reduce(
            jnp.logical_and, [ok & (w * ROWS >= start) for w, ok in zip(where, live)]
        )

        @pl.when(jnp.logical_not(alive))
        def _():
            if old is None:
                state[0][...] = jnp.full(state[0].shape, NEG, jnp.float32)
                state[1][...] = jnp.zeros(state[1].shape, jnp.float32)
                state[2][...] = jnp.zeros(state[2].shape, jnp.float32)
            else:
                for was, now in zip(old, state):
                    now[...] = was[...]

        def visit(masked):
            rows = base + lax.broadcasted_iota(jnp.int32, (ROWS, DIM), 0)
            rows_ok = start_of(rows, bounds) == start
            mask = None
            if masked:
                lane = lax.broadcasted_iota(jnp.int32, (1, ROWS), 1)
                mask = [(w * ROWS + lane >= start) & ok for w, ok in zip(where, live)]
            keys = [sets[i][pl.ds(o * 2 * ROWS, ROWS), :] for i, o, _ in places]
            values = [sets[i][pl.ds(o * 2 * ROWS + ROWS, ROWS), :] for i, o, _ in places]
            all_heads(q_ref, keys, values, mask, rows_ok, old, state)

        pl.when(whole)(lambda: visit(False))
        pl.when(alive & jnp.logical_not(whole))(lambda: visit(True))

    if pack:
        m_ref, l_ref, acc_ref = refs[:3]
        lane = lax.broadcasted_iota(jnp.int32, (ROWS, DIM), 1)
        stats = jnp.zeros((ROWS, DIM), jnp.float32)
        for h in range(HEADS):
            packed_ref[pl.ds(h * ROWS, ROWS), :] = acc_ref[h]
            stats = jnp.where(lane == h, m_ref[h], stats)
            stats = jnp.where(lane == HEADS + h, l_ref[h], stats)
        packed_ref[pl.ds(HEADS * ROWS, ROWS), :] = stats


def merge_kernel(m_ref, l_ref, acc_ref, packed_ref, out_ref):
    for h in range(HEADS):
        m2 = packed_ref[pl.ds(HEADS * ROWS, ROWS), h : h + 1]
        l2 = packed_ref[pl.ds(HEADS * ROWS, ROWS), HEADS + h : HEADS + h + 1]
        m1 = m_ref[h]
        top = jnp.maximum(m1, m2)
        keep, take = jnp.exp2((m1 - top) * SCALE), jnp.exp2((m2 - top) * SCALE)
        total = l_ref[h] * keep + l2 * take
        acc = acc_ref[h] * keep + packed_ref[pl.ds(h * ROWS, ROWS), :] * take
        out_ref[:, h * DIM : (h + 1) * DIM] = (acc / total).astype(jnp.bfloat16)


STATE = [jax.ShapeDtypeStruct((HEADS, ROWS, DIM), jnp.float32)] * 3
PACKED = jax.ShapeDtypeStruct(((HEADS + 1) * ROWS, DIM), jnp.float32)
PARAMS = pltpu.CompilerParams(vmem_limit_bytes=GRANT)


def price(blocks):
    pairs = HEADS * ROWS * ROWS * blocks
    return pl.CostEstimate(flops=4 * DIM * pairs, bytes_accessed=1 << 20, transcendentals=pairs)


def own_call(ids, q, kv):
    got = pl.pallas_call(
        own_kernel,
        out_shape=STATE + [jax.ShapeDtypeStruct((DOCS,), jnp.int32)],
        in_specs=[VM] * 3,
        out_specs=[VM] * 3 + [SM],
        compiler_params=PARAMS,
        cost_estimate=price(1),
        name="own",
    )(ids, q, kv)
    return got[:3], got[3]


def far_call(name, bounds, queries, sides, sets, places, states, pack=False):
    seeds = [state is None for state in states]
    flat = [a for state in states if state is not None for a in state]
    args = [*queries, *sets, *flat]
    out_shape = [PACKED] if pack else STATE * len(sides)
    got = pl.pallas_call(
        functools.partial(far_kernel, places, sides, seeds, pack),
        out_shape=out_shape,
        in_specs=[SM] + [VM] * len(args),
        out_specs=[VM] * len(out_shape),
        scratch_shapes=[pltpu.VMEM((HEADS, ROWS, DIM), jnp.float32)] * 3 if pack else [],
        compiler_params=PARAMS,
        cost_estimate=price(len(places) * len(sides)),
        name=name,
    )(bounds, *args)
    if pack:
        return got[0]
    return [got[3 * i : 3 * i + 3] for i in range(len(sides))]


def merge_call(state, packed):
    return pl.pallas_call(
        merge_kernel,
        out_shape=jax.ShapeDtypeStruct((ROWS, HEADS * DIM), jnp.bfloat16),
        in_specs=[VM] * 4,
        out_specs=VM,
        compiler_params=PARAMS,
        cost_estimate=pl.CostEstimate(flops=1 << 20, bytes_accessed=1 << 20, transcendentals=1 << 18),
        name="merge",
    )(*state, packed)


def back(chips):
    return lambda block: block - 2 * chips


def shift(array, chips):
    count = 2 * (SIDE * SIDE - chips)
    return lax.ppermute(array, "ctx", [(i, i + 2 * chips) for i in range(count)])


def swap(array):
    return lax.ppermute(array, "ctx", [(i, i ^ 1) for i in range(2 * SIDE * SIDE)])


def on_device(query_rows, key_rows, value_rows, document_ids):
    rows, ids = query_rows, document_ids.reshape(64, 128)
    top = lax.broadcasted_iota(jnp.int32, (2 * ROWS, DIM), 0) < ROWS
    own = jnp.where(
        top, jnp.pad(key_rows, ((0, ROWS), (0, 0))), jnp.pad(value_rows, ((ROWS, 0), (0, 0)))
    )
    near = {d: shift(own, d) for d in ORDER}
    other_rows = swap(rows)
    state, bounds = own_call(ids, rows, own)
    places = [(i, 0, back(d)) for i, d in enumerate((0,) + EARLY)]
    sets = [own] + [near[d] for d in EARLY]
    (other,) = far_call("early_o", bounds, [other_rows], (1,), sets, places, [None])
    places = [(i, 0, back(d)) for i, d in enumerate(EARLY)]
    (state,) = far_call("early", bounds, [rows], (0,), sets[1:], places, [state])
    state, other = lax.optimization_barrier((state, other))
    places = [(i, 0, back(d)) for i, d in enumerate(LATE)]
    sets = [near[d] for d in LATE]
    packed = far_call("late_o", bounds, [other_rows], (1,), sets, places, [other], True)
    packed = swap(packed)
    (state,) = far_call("late", bounds, [rows], (0,), sets, places, [state])
    return merge_call(state, packed)


def solution(mesh):
    in_specs = (P(("req", "ctx"), None), P(("req", "ctx"), None), P(("req", "ctx"), None), P("req"))
    out_specs = P(("req", "ctx"), None)
    return jax.shard_map(
        on_device, mesh=mesh, in_specs=in_specs, out_specs=out_specs, check_vma=False
    )
```

```python
import functools
import math

import jax
import jax.numpy as jnp
from jax import lax
from jax.experimental import pallas as pl
from jax.experimental.pallas import tpu as pltpu
from jax.sharding import PartitionSpec as P


HEADS = 8
DIM = 128
ROWS = 256
SIDE = 4
DOCS = 8
SCALE = math.log2(math.e) / math.sqrt(DIM)
NEG = -1e30
ORDER = ((4, 1), (5, 3), (8, 2), (6, 7))
GRANT = 32 << 20
VM = pl.BlockSpec(memory_space=pltpu.VMEM)


SM = pl.BlockSpec(memory_space=pltpu.SMEM)


def start_of(positions, bounds):
    start = jnp.zeros_like(positions)
    for b in bounds:
        start = jnp.where(positions >= b, jnp.maximum(start, b), start)
    return start


def score(q, keys, mask):
    scores = [
        lax.dot_general(q, k, (((1,), (1,)), ((), ())), preferred_element_type=jnp.float32)
        for k in keys
    ]
    if mask is None:
        return scores
    return [jnp.where(ok, s, NEG) for s, ok in zip(scores, mask)]


def absorb(h, scores, values, rows_ok, old_state, state, out_ref=None):
    top = jnp.max(functools.reduce(jnp.maximum, scores), axis=1, keepdims=True)
    if rows_ok is not None:
        top = jnp.where(rows_ok, top, NEG)
    if old_state is None:
        new = jnp.broadcast_to(top, (ROWS, DIM))
    else:
        old_m, old_l, old_acc = old_state
        old = old_m[h]
        new = jnp.maximum(old, top)
    cut = new * SCALE
    if rows_ok is not None:
        cut = jnp.where(rows_ok, cut, -NEG)
    wide = jnp.concatenate([cut] * (ROWS // DIM), axis=1)
    total = None
    for s, v in zip(scores, values):
        p = jnp.exp2(s * SCALE - wide).astype(jnp.bfloat16)
        part = jnp.dot(p, v, preferred_element_type=jnp.float32)
        total = part if total is None else total + part
    acc, sums = total[:, :DIM], total[:, DIM:]
    if old_state is not None:
        shrink = jnp.exp2((old - new) * SCALE)
        acc, sums = old_acc[h] * shrink + acc, old_l[h] * shrink + sums
    if out_ref is not None:
        out_ref[:, pl.ds(h * DIM, DIM)] = (acc / sums).astype(jnp.bfloat16)
        return
    m_ref, l_ref, acc_ref = state
    acc_ref[h] = acc
    l_ref[h] = sums
    m_ref[h] = new


def all_heads(q_ref, keys, values, mask, rows_ok, old_state, state, out_ref=None):
    values = [jnp.concatenate([v, jnp.ones_like(v)], axis=1) for v in values]

    def fill(h):
        return score(q_ref[:, h * DIM : (h + 1) * DIM], keys, mask)

    ahead = fill(0)
    for h in range(HEADS):
        now = ahead
        if h + 1 < HEADS:
            ahead = fill(h + 1)
        absorb(h, now, values, rows_ok, old_state, state, out_ref)


def own_kernel(ids_ref, q_ref, kv_ref, m_ref, l_ref, acc_ref, bounds_ref):
    block = lax.axis_index("ctx")
    base = block * ROWS
    ids = ids_ref[...]
    bounds = [jnp.sum((ids < d).astype(jnp.int32)) for d in range(1, DOCS)]
    for i, b in enumerate(bounds):
        bounds_ref[i] = b
    rows = base + lax.broadcasted_iota(jnp.int32, (ROWS, ROWS), 0)
    first = start_of(rows, bounds)
    keys, values, mask = [], [], []
    for i, w in enumerate((block, block + 1 - 2 * lax.rem(block, 2))):
        cols = w * ROWS + lax.broadcasted_iota(jnp.int32, (ROWS, ROWS), 1)
        mask.append((cols <= rows) & (cols >= first))
        keys.append(kv_ref[pl.ds(2 * i * ROWS, ROWS), :])
        values.append(kv_ref[pl.ds((2 * i + 1) * ROWS, ROWS), :])
    all_heads(q_ref, keys, values, mask, None, None, (m_ref, l_ref, acc_ref))


def far_kernel(places, last, bounds_ref, q_ref, *refs):
    n = 1 + max(i for i, _, _ in places)
    sets, old, refs = refs[:n], refs[n : n + 3], refs[n + 3 :]
    out_ref, state = (refs[0], None) if last else (None, refs)
    block = lax.axis_index("ctx")
    bounds = [bounds_ref[i] for i in range(DOCS - 1)]
    base = block * ROWS
    start = start_of(base, bounds)
    where = [jnp.int32(blk(block)) for _, _, blk in places]
    live = [(w >= 0) & (w < block) & (w * ROWS + ROWS > start) for w in where]
    alive = functools.reduce(jnp.logical_or, live)
    whole = functools.reduce(
        jnp.logical_and, [ok & (w * ROWS >= start) for w, ok in zip(where, live)]
    )

    @pl.when(jnp.logical_not(alive))
    def _():
        if last:
            _, l_ref, acc_ref = old
            for h in range(HEADS):
                out_ref[:, pl.ds(h * DIM, DIM)] = (acc_ref[h] / l_ref[h]).astype(jnp.bfloat16)
        else:
            for was, now in zip(old, state):
                now[...] = was[...]

    def visit(masked):
        rows = base + lax.broadcasted_iota(jnp.int32, (ROWS, DIM), 0)
        rows_ok = start_of(rows, bounds) == start
        mask = None
        if masked:
            lane = lax.broadcasted_iota(jnp.int32, (1, ROWS), 1)
            mask = [(w * ROWS + lane >= start) & ok for w, ok in zip(where, live)]
        keys = [sets[i][pl.ds(o * 2 * ROWS, ROWS), :] for i, o, _ in places]
        values = [sets[i][pl.ds(o * 2 * ROWS + ROWS, ROWS), :] for i, o, _ in places]
        all_heads(q_ref, keys, values, mask, rows_ok, old, state, out_ref)

    pl.when(whole)(lambda: visit(False))
    pl.when(alive & jnp.logical_not(whole))(lambda: visit(True))


STATE = [jax.ShapeDtypeStruct((HEADS, ROWS, DIM), jnp.float32)] * 3
PARAMS = pltpu.CompilerParams(vmem_limit_bytes=GRANT)


def price(blocks):
    pairs = HEADS * ROWS * ROWS * blocks
    return pl.CostEstimate(flops=4 * DIM * pairs, bytes_accessed=1 << 20, transcendentals=pairs)


def own_call(ids, q, kv):
    got = pl.pallas_call(
        own_kernel,
        out_shape=STATE + [jax.ShapeDtypeStruct((DOCS,), jnp.int32)],
        in_specs=[VM] * 3,
        out_specs=[VM] * 3 + [SM],
        compiler_params=PARAMS,
        cost_estimate=price(1),
        name="own",
    )(ids, q, kv)
    return got[:3], got[3]


def far_call(bounds, q, sets, places, state, last=False):
    args = [q, *sets, *state]
    out_shape = [jax.ShapeDtypeStruct(q.shape, q.dtype)] if last else STATE
    got = pl.pallas_call(
        functools.partial(far_kernel, places, last),
        out_shape=out_shape,
        in_specs=[SM] + [VM] * len(args),
        out_specs=[VM] * len(out_shape),
        compiler_params=PARAMS,
        cost_estimate=price(len(places)),
    )(bounds, *args)
    return got[0] if last else got


def came(first, second, second_half, other):
    def blk(block):
        chip, core = lax.div(block, 2), lax.rem(block, 2)
        core = 1 - core if other else core
        chip = chip - jnp.where(core == 0, first, second)
        return 2 * chip + (1 - core if second_half else core)

    return blk


def shift(array, first, second):
    chips = SIDE * SIDE
    pairs = [(2 * i, 2 * (i + first)) for i in range(chips - first)]
    pairs += [(2 * i + 1, 2 * (i + second) + 1) for i in range(chips - second)]
    return lax.ppermute(array, "ctx", pairs)


def swap(array):
    return lax.ppermute(array, "ctx", [(i, i ^ 1) for i in range(2 * SIDE * SIDE)])


def on_device(query_rows, key_rows, value_rows, document_ids):
    rows, ids = query_rows, document_ids.reshape(64, 128)
    top = lax.broadcasted_iota(jnp.int32, (2 * ROWS, DIM), 0) < ROWS
    own = jnp.where(
        top, jnp.pad(key_rows, ((0, ROWS), (0, 0))), jnp.pad(value_rows, ((ROWS, 0), (0, 0)))
    )
    chip = jnp.concatenate([own, swap(own)], axis=0)
    got = []
    for a, b in ORDER:
        got.append(shift(chip, a, b))
    state, bounds = own_call(ids, rows, chip)
    for name, use in (("far", (0, 1)), ("end", (2, 3))):
        both = jnp.concatenate([got[j] for j in use], axis=0)
        sets = [got[j] for j in use] + [swap(both)]
        places = [(i, o, came(*ORDER[j], o, False)) for i, j in enumerate(use) for o in range(2)]
        places += [
            (2, 2 * i + o, came(*ORDER[j], o, True)) for i, j in enumerate(use) for o in range(2)
        ]
        state = far_call(bounds, rows, sets, places, state, name == "end")
    return state


def solution(mesh):
    in_specs = (P(("req", "ctx"), None), P(("req", "ctx"), None), P(("req", "ctx"), None), P("req"))
    out_specs = P(("req", "ctx"), None)
    return jax.shard_map(
        on_device, mesh=mesh, in_specs=in_specs, out_specs=out_specs, check_vma=False
    )
```
